32 devices in a mesh: row: 4 (over z), col: 8 (over y, x, core).
Axes of the slice: x: 2, y: 2, z: 4, core: 2. Of those that a mesh axis runs over, the one named last changes fastest.
Arguments:
- pair: bfloat16 [128, 128, 128], P('row', 'col'), may hold values from -6 to 6
- gain_in: float32 [128], replicated, may hold values from 0.1 to 1.9
- w_left_gate: bfloat16 [128, 128], replicated, may hold values from -0.5 to 0.5
- w_left: bfloat16 [128, 128], replicated, may hold values from -0.5 to 0.5
- w_right_gate: bfloat16 [128, 128], replicated, may hold values from -0.5 to 0.5
- w_right: bfloat16 [128, 128], replicated, may hold values from -0.5 to 0.5
- gain_out: float32 [128], replicated, may hold values from 0.1 to 1.9
- w_out_gate: bfloat16 [128, 128], replicated, may hold values from -0.5 to 0.5
- w_out: bfloat16 [128, 128], replicated, may hold values from -0.5 to 0.5
Outputs:
- update: bfloat16 [128, 128, 128], P('row', 'col')
The draws below stay inside these ranges and needn't reach their ends.
All inputs are finite; a program needn't handle non-finite values.
Results may differ from the reference program's by a relative error of at most 0.0081.
Values may be sent and summed in bfloat16 or wider, within the bound.
A program may use at most 64 MiB of HBM per device.

```python
import jax
import jax.numpy as jnp
from jax import lax

C = 128
H = 128
N = 128


def levels(stream_key, shape, cuts, low, high):
    def one(axis_at, blocks):
        draws = jax.random.uniform(jax.random.fold_in(jax.random.fold_in(stream_key, 6), axis_at), (blocks,), jnp.float32, low / len(cuts), high / len(cuts))
        return jnp.repeat(jnp.exp(draws), shape[axis_at] // blocks).reshape((-1,) + (1,) * (len(shape) - axis_at - 1))

    loudness = one(*cuts[0])
    for cut in cuts[1:]:
        loudness = loudness * one(*cut)
    return loudness


def gaussian(key, shape, spread, most, shards=(), kind=jnp.bfloat16):
    entries = spread * jax.random.normal(key, shape, jnp.float32)
    if shards:
        entries = entries * levels(key, shape, shards, -0.22, 0.18)
    return jnp.clip(entries, -most, most).astype(kind)


def setup_inputs(seed: int = 0) -> dict:
    arg_keys = jax.random.split(jax.random.key(seed), 10)
    return {
        "pair": gaussian(arg_keys[0], (N, N, C), 1.0, 6.0, ((0, 4), (1, 8))),
        "gain_in": jnp.clip(1.0 + 0.18 * jax.random.normal(arg_keys[1], (C,), jnp.float32), 0.1, 1.9),
        "w_left_gate": gaussian(arg_keys[2], (C, H), C ** -0.5, 0.5),
        "w_left": gaussian(arg_keys[3], (C, H), C ** -0.5, 0.5),
        "w_right_gate": gaussian(arg_keys[4], (C, H), C ** -0.5, 0.5),
        "w_right": gaussian(arg_keys[5], (C, H), C ** -0.5, 0.5),
        "gain_out": jnp.clip(1.0 + 0.18 * jax.random.normal(arg_keys[6], (H,), jnp.float32), 0.1, 1.9),
        "w_out_gate": gaussian(arg_keys[7], (C, C), C ** -0.5, 0.5),
        "w_out": gaussian(arg_keys[8], (H, C), H ** -0.5, 0.5),
    }


def layer_norm(values, gain):
    mean = lax.optimization_barrier(jnp.mean(values, axis=-1, keepdims=True))
    centred = values - mean
    variance = lax.optimization_barrier(jnp.mean(centred * centred, axis=-1, keepdims=True))
    return centred * jax.lax.rsqrt(variance + 1e-05) * gain

def project(normed, weight):
    return jnp.einsum('ijc,ch->ijh', normed.astype(jnp.float32), weight.astype(jnp.float32))

def reference(pair, gain_in, w_left_gate, w_left, w_right_gate, w_right, gain_out, w_out_gate, w_out):
    normed = layer_norm(pair.astype(jnp.float32), gain_in.astype(jnp.float32)).astype(jnp.bfloat16)
    left = (jax.nn.sigmoid(project(normed, w_left_gate)) * project(normed, w_left)).astype(jnp.bfloat16)
    right = (jax.nn.sigmoid(project(normed, w_right_gate)) * project(normed, w_right)).astype(jnp.bfloat16)
    mixed = jnp.einsum('ikh,jkh->ijh', left.astype(jnp.float32), right.astype(jnp.float32))
    out_normed = layer_norm(mixed, gain_out.astype(jnp.float32)).astype(jnp.bfloat16)
    gate = jax.nn.sigmoid(project(normed, w_out_gate))
    return (gate * project(out_normed, w_out)).astype(jnp.bfloat16)
```

```python
import functools

import jax
import jax.numpy as jnp
from jax import lax
from jax.experimental import pallas as pl
from jax.experimental.pallas import tpu as pltpu
from jax.sharding import PartitionSpec as P

MESH = pl.DeviceIdType.MESH
F32 = jnp.float32
BF16 = jnp.bfloat16
GROUP = 8


def layer_norm(values, gain):
    mean = jnp.mean(values, axis=-1, keepdims=True)
    centred = values - mean
    variance = jnp.mean(centred * centred, axis=-1, keepdims=True)
    return centred * lax.rsqrt(variance + 1e-05) * gain


def gated(normed, w_gate, w):
    gate = jnp.dot(normed, w_gate, preferred_element_type=F32)
    value = jnp.dot(normed, w, preferred_element_type=F32)
    return (jax.nn.sigmoid(gate) * value).astype(BF16)


def kernel(
    nr, nc,
    pair, gain_in, w_left_gate, w_left, w_right_gate, w_right, gain_out, w_out_gate, w_out,
    out,
    normed_f, normed_t, gate, left_buf, right_own, right_buf, left_f, acc,
    left_send, left_fwd, left_recv, right_send, right_recv,
):
    rows, cols, width = pair.shape
    ratio = nc // nr
    chips = nc // 2
    r = lax.axis_index("row")
    c = lax.axis_index("col")
    chip, core = c // 2, c % 2
    sibling = chip * 2 + 1 - core
    home = c // ratio

    def same_core(a):
        return (chip + a) % chips * 2 + core

    def other_core(a):
        return (chip + a) % chips * 2 + 1 - core

    barrier = pltpu.get_barrier_semaphore()
    def greet(row, col):
        pl.semaphore_signal(barrier, inc=1, device_id={"row": row, "col": col}, device_id_type=MESH)
    greet(r, sibling)
    for a in range(1, chips):
        greet(r, same_core(a))
    for s in range(1, nc):
        greet(home, (c + s) % nc)
    @pl.when(home != r)
    def _():
        greet(home, c)

    normed = layer_norm(pair[...].reshape(rows * cols, width).astype(F32), gain_in[...])
    normed_f[...] = normed
    normed = normed.astype(BF16)
    left_buf[c] = gated(normed, w_left_gate[...], w_left[...])
    for t in range(ratio):
        for k in range(cols):
            normed_t[pl.ds((t * cols + k) * cols, cols), :] = normed_f[
                pl.ds(t * cols * cols + k, cols, stride=cols), :
            ].astype(BF16)
    right = gated(normed_t[...], w_right_gate[...], w_right[...])
    right_own[...] = right.reshape(ratio, cols, cols, width)

    left_peers = chips
    total = left_peers + nr * ratio
    self_right = (home == r).astype(jnp.int32)
    pl.semaphore_wait(barrier, total - self_right)

    def left_copy(block, col, sem):
        return pltpu.make_async_remote_copy(
            src_ref=left_buf.at[block], dst_ref=left_buf.at[block],
            send_sem=sem, recv_sem=left_recv.at[block],
            device_id={"row": r, "col": col}, device_id_type=MESH,
        )

    def right_copy(dz, t):
        return pltpu.make_async_remote_copy(
            src_ref=right_own.at[t], dst_ref=right_buf.at[c],
            send_sem=right_send.at[dz * ratio + t], recv_sem=right_recv.at[c],
            device_id={"row": (r + dz) % nr, "col": r * ratio + t}, device_id_type=MESH,
        )

    def right_local(t):
        return pltpu.make_async_copy(right_own.at[t], right_buf.at[c], right_recv.at[c])

    for a in range(1, chips):
        left_copy(c, same_core(a), left_send.at[a]).start()
    left_copy(c, sibling, left_send.at[0]).start()
    for dz in list(range(1, nr)) + [0]:
        for t in range(ratio):
            if dz:
                right_copy(dz, t).start()
            else:
                here = r * ratio + t == c
                @pl.when(here)
                def _(t=t):
                    right_local(t).start()
                @pl.when(jnp.logical_not(here))
                def _(t=t):
                    right_copy(0, t).start()

    gate[...] = jax.nn.sigmoid(jnp.dot(normed, w_out_gate[...], preferred_element_type=F32))
    acc[...] = jnp.zeros_like(acc)

    for a in range(1, chips):
        block = same_core(a)
        left_copy(block, sibling, left_fwd.at[a]).wait_recv()
        left_copy(block, sibling, left_fwd.at[a]).start()

    def mix(block):
        pltpu.make_async_remote_copy(
            src_ref=right_own.at[0], dst_ref=right_buf.at[block],
            send_sem=right_send.at[0], recv_sem=right_recv.at[block],
            device_id={"row": r, "col": sibling}, device_id_type=MESH,
        ).wait_recv()
        left_f[...] = left_buf[block].astype(F32).reshape(rows, cols, width)

        def group(g, carry):
            sums = [acc[g * GROUP + n] for n in range(GROUP)]
            for k in range(cols):
                other = right_buf[block, k].astype(F32)
                for n in range(GROUP):
                    sums[n] = sums[n] + left_f[g * GROUP + n, pl.ds(k, 1), :] * other
            for n in range(GROUP):
                acc[g * GROUP + n] = sums[n]
            return carry

        lax.fori_loop(0, rows // GROUP, group, 0)

    def own_core(a, carry):
        mix(same_core(a))
        return carry

    def their_core(a, carry):
        block = other_core(a)
        left_copy(block, sibling, left_send.at[0]).wait_recv()
        mix(block)
        return carry

    lax.fori_loop(0, chips, own_core, 0)
    lax.fori_loop(0, chips, their_core, 0)

    mixed = acc[...].reshape(rows * cols, width)
    out_normed = layer_norm(mixed, gain_out[...]).astype(BF16)
    update = gate[...] * jnp.dot(out_normed, w_out[...], preferred_element_type=F32)
    out[...] = update.astype(BF16).reshape(rows, cols, width)

    left_copy(c, sibling, left_send.at[0]).wait_send()
    for a in range(1, chips):
        left_copy(c, same_core(a), left_send.at[a]).wait_send()
        left_copy(same_core(a), sibling, left_fwd.at[a]).wait_send()
    for dz in range(nr):
        for t in range(ratio):
            if dz:
                right_copy(dz, t).wait_send()
            else:
                @pl.when(r * ratio + t != c)
                def _(t=t):
                    right_copy(0, t).wait_send()


def solution(mesh):
    nr, nc = mesh.shape["row"], mesh.shape["col"]

    def per_device(
        pair, gain_in, w_left_gate, w_left, w_right_gate, w_right, gain_out, w_out_gate, w_out
    ):
        rows, cols, width = pair.shape
        flat = rows * cols
        ratio = nc // nr
        dma = pltpu.SemaphoreType.DMA
        return pl.pallas_call(
            functools.partial(kernel, nr, nc),
            out_shape=jax.ShapeDtypeStruct(pair.shape, BF16),
            in_specs=[pl.BlockSpec(memory_space=pltpu.VMEM)] * 9,
            out_specs=pl.BlockSpec(memory_space=pltpu.VMEM),
            scratch_shapes=[
                pltpu.VMEM((flat, width), F32),
                pltpu.VMEM((flat, width), BF16),
                pltpu.VMEM((flat, width), F32),
                pltpu.VMEM((nc, flat, width), BF16),
                pltpu.VMEM((ratio, cols, cols, width), BF16),
                pltpu.VMEM((nc, cols, cols, width), BF16),
                pltpu.VMEM((rows, cols, width), F32),
                pltpu.VMEM((rows, cols, width), F32),
                dma((nc // 2,)),
                dma((nc // 2,)),
                dma((nc,)),
                dma((nr * ratio,)),
                dma((nc,)),
            ],
            compiler_params=pltpu.CompilerParams(collective_id=0, has_side_effects=True),
        )(
            pair, gain_in.reshape(1, -1), w_left_gate, w_left, w_right_gate, w_right,
            gain_out.reshape(1, -1), w_out_gate, w_out,
        )

    return jax.shard_map(
        per_device,
        mesh=mesh,
        in_specs=(P("row", "col", None), P(), P(), P(), P(), P(), P(), P(), P()),
        out_specs=P("row", "col", None),
        check_vma=False,
    )
```

```python
import functools

import jax
import jax.numpy as jnp
from jax import lax
from jax.experimental import pallas as pl
from jax.experimental.pallas import tpu as pltpu
from jax.sharding import PartitionSpec as P

MESH = pl.DeviceIdType.MESH
F32 = jnp.float32
BF16 = jnp.bfloat16
GROUP = 8


def layer_norm(values, gain):
    mean = jnp.mean(values, axis=-1, keepdims=True)
    centred = values - mean
    variance = jnp.mean(centred * centred, axis=-1, keepdims=True)
    return centred * lax.rsqrt(variance + 1e-05) * gain


def gated(normed, w_gate, w):
    gate = jnp.dot(normed, w_gate, preferred_element_type=F32)
    value = jnp.dot(normed, w, preferred_element_type=F32)
    return (jax.nn.sigmoid(gate) * value).astype(BF16)


def kernel(
    nr, nc,
    pair, gain_in, w_left_gate, w_left, w_right_gate, w_right, gain_out, w_out_gate, w_out,
    out,
    normed_f, normed_t, gate, left_buf, chain, right_buf, left_f, acc,
    left_send, left_fwd, left_recv, right_send, right_recv, up_send, down_send, chain_recv,
):
    rows, cols, width = pair.shape
    ratio = nc // nr
    chips = nc // 2
    r = lax.axis_index("row")
    c = lax.axis_index("col")
    chip, core = c // 2, c % 2
    sibling = chip * 2 + 1 - core

    def same_core(a):
        return (chip + a) % chips * 2 + core

    def other_core(a):
        return (chip + a) % chips * 2 + 1 - core

    barrier = pltpu.get_barrier_semaphore()

    def greet(row, col):
        pl.semaphore_signal(barrier, inc=1, device_id={"row": row, "col": col}, device_id_type=MESH)

    for s in range(1, nc):
        greet(r, (c + s) % nc)

    @pl.when(r > 0)
    def _():
        greet(r - 1, c)

    @pl.when(r < nr - 1)
    def _():
        greet(r + 1, c)

    def chain_copy(block, t, row, sem):
        return pltpu.make_async_remote_copy(
            src_ref=chain.at[block, t], dst_ref=chain.at[block, t],
            send_sem=sem, recv_sem=chain_recv.at[block, t],
            device_id={"row": row, "col": c}, device_id_type=MESH,
        )

    def right_copy(block, t):
        return pltpu.make_async_remote_copy(
            src_ref=chain.at[block, t], dst_ref=right_buf.at[c],
            send_sem=right_send.at[block, t], recv_sem=right_recv.at[c],
            device_id={"row": r, "col": block * ratio + t}, device_id_type=MESH,
        )

    def left_copy(block, col, sem):
        return pltpu.make_async_remote_copy(
            src_ref=left_buf.at[block], dst_ref=left_buf.at[block],
            send_sem=sem, recv_sem=left_recv.at[block],
            device_id={"row": r, "col": col}, device_id_type=MESH,
        )

    def deliver(block, t):
        here = block * ratio + t == c

        @pl.when(here)
        def _():
            pltpu.make_async_copy(chain.at[block, t], right_buf.at[c], right_recv.at[c]).start()

        @pl.when(jnp.logical_not(here))
        def _():
            right_copy(block, t).start()

    normed = layer_norm(pair[...].reshape(rows * cols, width).astype(F32), gain_in[...])
    normed_f[...] = normed
    for t in range(ratio):
        for k in range(cols):
            normed_t[pl.ds((t * cols + k) * cols, cols), :] = normed_f[
                pl.ds(t * cols * cols + k, cols, stride=cols), :
            ].astype(BF16)
    right = gated(normed_t[...], w_right_gate[...], w_right[...])
    chain[r] = right.reshape(ratio, cols, cols, width)

    pl.semaphore_wait(
        barrier, nc - 1 + (r > 0).astype(jnp.int32) + (r < nr - 1).astype(jnp.int32)
    )

    for t in range(ratio):
        @pl.when(r < nr - 1)
        def _(t=t):
            chain_copy(r, t, r + 1, up_send.at[r, t]).start()

        @pl.when(r > 0)
        def _(t=t):
            chain_copy(r, t, r - 1, down_send.at[r, t]).start()

    normed = normed.astype(BF16)
    left_buf[c] = gated(normed, w_left_gate[...], w_left[...])
    for t in range(ratio):
        deliver(r, t)
    for a in range(1, chips):
        left_copy(c, same_core(a), left_send.at[a]).start()
    left_copy(c, sibling, left_send.at[0]).start()

    gate[...] = jax.nn.sigmoid(jnp.dot(normed, w_out_gate[...], preferred_element_type=F32))
    acc[...] = jnp.zeros_like(acc)

    def relay(d):
        for t in range(ratio):
            @pl.when(r - d >= 0)
            def _(t=t):
                block = r - d
                chain_copy(block, t, r, up_send.at[block, t]).wait_recv()

                @pl.when(r < nr - 1)
                def _():
                    chain_copy(block, t, r + 1, up_send.at[block, t]).start()

                deliver(block, t)

            @pl.when(r + d < nr)
            def _(t=t):
                block = r + d
                chain_copy(block, t, r, down_send.at[block, t]).wait_recv()

                @pl.when(r > 0)
                def _():
                    chain_copy(block, t, r - 1, down_send.at[block, t]).start()

                deliver(block, t)

    for d in range(1, nr - 1):
        relay(d)
    for a in range(1, chips):
        block = same_core(a)
        left_copy(block, sibling, left_fwd.at[a]).wait_recv()
        left_copy(block, sibling, left_fwd.at[a]).start()
    relay(nr - 1)

    def mix(block):
        pltpu.make_async_remote_copy(
            src_ref=chain.at[0, 0], dst_ref=right_buf.at[block],
            send_sem=right_send.at[0, 0], recv_sem=right_recv.at[block],
            device_id={"row": r, "col": sibling}, device_id_type=MESH,
        ).wait_recv()
        left_f[...] = left_buf[block].astype(F32).reshape(rows, cols, width)

        def group(g, carry):
            sums = [acc[g * GROUP + n] for n in range(GROUP)]
            for k in range(cols):
                other = right_buf[block, k].astype(F32)
                for n in range(GROUP):
                    sums[n] = sums[n] + left_f[g * GROUP + n, pl.ds(k, 1), :] * other
            for n in range(GROUP):
                acc[g * GROUP + n] = sums[n]
            return carry

        lax.fori_loop(0, rows // GROUP, group, 0)

    def own_core(a, carry):
        mix(same_core(a))
        return carry

    def their_core(a, carry):
        block = other_core(a)
        left_copy(block, sibling, left_send.at[0]).wait_recv()
        mix(block)
        return carry

    lax.fori_loop(0, chips, own_core, 0)
    lax.fori_loop(0, chips, their_core, 0)

    mixed = acc[...].reshape(rows * cols, width)
    out_normed = layer_norm(mixed, gain_out[...]).astype(BF16)
    update = gate[...] * jnp.dot(out_normed, w_out[...], preferred_element_type=F32)
    out[...] = update.astype(BF16).reshape(rows, cols, width)

    left_copy(c, sibling, left_send.at[0]).wait_send()
    for a in range(1, chips):
        left_copy(c, same_core(a), left_send.at[a]).wait_send()
        left_copy(same_core(a), sibling, left_fwd.at[a]).wait_send()
    for block in range(nr):
        for t in range(ratio):
            @pl.when(block * ratio + t != c)
            def _(block=block, t=t):
                right_copy(block, t).wait_send()

            @pl.when(jnp.logical_and(r >= block, r < nr - 1))
            def _(block=block, t=t):
                chain_copy(block, t, r + 1, up_send.at[block, t]).wait_send()

            @pl.when(jnp.logical_and(r <= block, r > 0))
            def _(block=block, t=t):
                chain_copy(block, t, r - 1, down_send.at[block, t]).wait_send()


def solution(mesh):
    nr, nc = mesh.shape["row"], mesh.shape["col"]

    def per_device(
        pair, gain_in, w_left_gate, w_left, w_right_gate, w_right, gain_out, w_out_gate, w_out
    ):
        rows, cols, width = pair.shape
        flat = rows * cols
        ratio = nc // nr
        dma = pltpu.SemaphoreType.DMA
        return pl.pallas_call(
            functools.partial(kernel, nr, nc),
            out_shape=jax.ShapeDtypeStruct(pair.shape, BF16),
            in_specs=[pl.BlockSpec(memory_space=pltpu.VMEM)] * 9,
            out_specs=pl.BlockSpec(memory_space=pltpu.VMEM),
            scratch_shapes=[
                pltpu.VMEM((flat, width), F32),
                pltpu.VMEM((flat, width), BF16),
                pltpu.VMEM((flat, width), F32),
                pltpu.VMEM((nc, flat, width), BF16),
                pltpu.VMEM((nr, ratio, cols, cols, width), BF16),
                pltpu.VMEM((nc, cols, cols, width), BF16),
                pltpu.VMEM((rows, cols, width), F32),
                pltpu.VMEM((rows, cols, width), F32),
                dma((nc // 2,)),
                dma((nc // 2,)),
                dma((nc,)),
                dma((nr, ratio)),
                dma((nc,)),
                dma((nr, ratio)),
                dma((nr, ratio)),
                dma((nr, ratio)),
            ],
            compiler_params=pltpu.CompilerParams(collective_id=0, has_side_effects=True),
        )(
            pair, gain_in.reshape(1, -1), w_left_gate, w_left, w_right_gate, w_right,
            gain_out.reshape(1, -1), w_out_gate, w_out,
        )

    return jax.shard_map(
        per_device,
        mesh=mesh,
        in_specs=(P("row", "col", None), P(), P(), P(), P(), P(), P(), P(), P()),
        out_specs=P("row", "col", None),
        check_vma=False,
    )
```

```python
import functools

import jax
import jax.numpy as jnp
from jax import lax
from jax.experimental import pallas as pl
from jax.experimental.pallas import tpu as pltpu
from jax.sharding import PartitionSpec as P

MESH = pl.DeviceIdType.MESH
F32 = jnp.float32
BF16 = jnp.bfloat16
GROUP = 8
PIECES = 1


def layer_norm(values, gain):
    mean = jnp.mean(values, axis=-1, keepdims=True)
    centred = values - mean
    variance = jnp.mean(centred * centred, axis=-1, keepdims=True)
    return centred * lax.rsqrt(variance + 1e-05) * gain


def gated(normed, w_gate, w):
    gate = jnp.dot(normed, w_gate, preferred_element_type=F32)
    value = jnp.dot(normed, w, preferred_element_type=F32)
    return (jax.nn.sigmoid(gate) * value).astype(BF16)


def kernel(
    nr, nc,
    pair, gain_in, w_left_gate, w_left, w_right_gate, w_right, gain_out, w_out_gate, w_out,
    out,
    normed_f, normed_t, gate, left_buf, chain, right_buf, left_f, acc,
    left_send, left_fwd, left_recv, right_send, right_recv, up_send, down_send, chain_recv,
):
    rows, cols, width = pair.shape
    ratio = nc // nr
    chips = nc // 2
    r = lax.axis_index("row")
    c = lax.axis_index("col")
    chip, core = c // 2, c % 2
    depth = cols // PIECES
    parts = [(t, u) for u in range(PIECES) for t in range(ratio)]
    sibling = chip * 2 + 1 - core

    def same_core(a):
        return (chip + a) % chips * 2 + core

    def other_core(a):
        return (chip + a) % chips * 2 + 1 - core

    barrier = pltpu.get_barrier_semaphore()

    def greet(row, col):
        pl.semaphore_signal(barrier, inc=1, device_id={"row": row, "col": col}, device_id_type=MESH)

    for s in range(1, nc):
        greet(r, (c + s) % nc)

    @pl.when(r > 0)
    def _():
        greet(r - 1, c)

    @pl.when(r < nr - 1)
    def _():
        greet(r + 1, c)

    def chain_copy(block, t, u, row, sem):
        piece = chain.at[block, t, pl.ds(u * depth, depth)]
        return pltpu.make_async_remote_copy(
            src_ref=piece, dst_ref=piece, send_sem=sem.at[block, t, u],
            recv_sem=chain_recv.at[block, t, u],
            device_id={"row": row, "col": c}, device_id_type=MESH,
        )

    def right_copy(block, t, u):
        return pltpu.make_async_remote_copy(
            src_ref=chain.at[block, t, pl.ds(u * depth, depth)],
            dst_ref=right_buf.at[c, pl.ds(u * depth, depth)],
            send_sem=right_send.at[block, t, u], recv_sem=right_recv.at[c, u],
            device_id={"row": r, "col": block * ratio + t}, device_id_type=MESH,
        )

    def left_copy(block, col, sem):
        return pltpu.make_async_remote_copy(
            src_ref=left_buf.at[block], dst_ref=left_buf.at[block],
            send_sem=sem, recv_sem=left_recv.at[block],
            device_id={"row": r, "col": col}, device_id_type=MESH,
        )

    def deliver(block, t, u):
        here = block * ratio + t == c

        @pl.when(here)
        def _():
            pltpu.make_async_copy(
                chain.at[block, t, pl.ds(u * depth, depth)],
                right_buf.at[c, pl.ds(u * depth, depth)],
                right_recv.at[c, u],
            ).start()

        @pl.when(jnp.logical_not(here))
        def _():
            right_copy(block, t, u).start()

    normed = layer_norm(pair[...].reshape(rows * cols, width).astype(F32), gain_in[...])
    normed_f[...] = normed
    for t, u in parts:
        for k in range(cols):
            normed_t[pl.ds((t * cols + k) * cols, cols), :] = normed_f[
                pl.ds(t * cols * cols + k, cols, stride=cols), :
            ].astype(BF16)
        block = normed_t[pl.ds(t * cols * cols, cols * cols), :]
        right = gated(block, w_right_gate[...], w_right[...])
        chain[r, t] = right.reshape(cols, cols, width)
        if t == 0:
            pl.semaphore_wait(
                barrier, nc - 1 + (r > 0).astype(jnp.int32) + (r < nr - 1).astype(jnp.int32)
            )

        @pl.when(r < nr - 1)
        def _(t=t, u=u):
            chain_copy(r, t, u, r + 1, up_send).start()

        @pl.when(r > 0)
        def _(t=t, u=u):
            chain_copy(r, t, u, r - 1, down_send).start()

    normed = normed.astype(BF16)
    left_buf[c] = gated(normed, w_left_gate[...], w_left[...])
    for a in range(1, chips):
        left_copy(c, same_core(a), left_send.at[a]).start()
    left_copy(c, sibling, left_send.at[0]).start()

    for t, u in parts:
        deliver(r, t, u)
    gate[...] = jax.nn.sigmoid(jnp.dot(normed, w_out_gate[...], preferred_element_type=F32))
    acc[...] = jnp.zeros_like(acc)

    def widen(block):
        left_f[block] = left_buf[block].astype(F32).reshape(rows, cols, width)

    widen(c)

    def relay(d):
        for t, u in parts:
            @pl.when(r - d >= 0)
            def _(t=t, u=u):
                block = r - d
                chain_copy(block, t, u, r, up_send).wait_recv()

                @pl.when(r < nr - 1)
                def _():
                    chain_copy(block, t, u, r + 1, up_send).start()

                deliver(block, t, u)

            @pl.when(r + d < nr)
            def _(t=t, u=u):
                block = r + d
                chain_copy(block, t, u, r, down_send).wait_recv()

                @pl.when(r > 0)
                def _():
                    chain_copy(block, t, u, r - 1, down_send).start()

                deliver(block, t, u)

    for d in range(1, nr - 1):
        relay(d)
    for a in range(1, chips):
        block = same_core(a)
        left_copy(block, sibling, left_fwd.at[a]).wait_recv()
        left_copy(block, sibling, left_fwd.at[a]).start()
        widen(block)
    relay(nr - 1)
    for a in range(chips):
        block = other_core(a)
        left_copy(block, sibling, left_send.at[0]).wait_recv()
        widen(block)

    def mix(block, u):
        pltpu.make_async_remote_copy(
            src_ref=chain.at[0, 0, pl.ds(0, depth)],
            dst_ref=right_buf.at[block, pl.ds(u * depth, depth)],
            send_sem=right_send.at[0, 0, 0], recv_sem=right_recv.at[block, u],
            device_id={"row": r, "col": sibling}, device_id_type=MESH,
        ).wait_recv()

        def group(g, carry):
            sums = [acc[g * GROUP + n] for n in range(GROUP)]
            for k in range(u * depth, (u + 1) * depth):
                other = right_buf[block, k].astype(F32)
                for n in range(GROUP):
                    sums[n] = sums[n] + left_f[block, g * GROUP + n, pl.ds(k, 1), :] * other
            for n in range(GROUP):
                acc[g * GROUP + n] = sums[n]
            return carry

        lax.fori_loop(0, rows // GROUP, group, 0)

    for u in range(PIECES):
        def step(s, carry, u=u):
            mix((chip + s // 2) % chips * 2 + (core + s) % 2, u)
            return carry

        lax.fori_loop(0, nc, step, 0)

    mixed = acc[...].reshape(rows * cols, width)
    out_normed = layer_norm(mixed, gain_out[...]).astype(BF16)
    update = gate[...] * jnp.dot(out_normed, w_out[...], preferred_element_type=F32)
    out[...] = update.astype(BF16).reshape(rows, cols, width)

    left_copy(c, sibling, left_send.at[0]).wait_send()
    for a in range(1, chips):
        left_copy(c, same_core(a), left_send.at[a]).wait_send()
        left_copy(same_core(a), sibling, left_fwd.at[a]).wait_send()
    for block in range(nr):
        for t, u in parts:
            @pl.when(block * ratio + t != c)
            def _(block=block, t=t, u=u):
                right_copy(block, t, u).wait_send()

            @pl.when(jnp.logical_and(r >= block, r < nr - 1))
            def _(block=block, t=t, u=u):
                chain_copy(block, t, u, r + 1, up_send).wait_send()

            @pl.when(jnp.logical_and(r <= block, r > 0))
            def _(block=block, t=t, u=u):
                chain_copy(block, t, u, r - 1, down_send).wait_send()


def solution(mesh):
    nr, nc = mesh.shape["row"], mesh.shape["col"]

    def per_device(
        pair, gain_in, w_left_gate, w_left, w_right_gate, w_right, gain_out, w_out_gate, w_out
    ):
        rows, cols, width = pair.shape
        flat = rows * cols
        ratio = nc // nr
        dma = pltpu.SemaphoreType.DMA
        return pl.pallas_call(
            functools.partial(kernel, nr, nc),
            out_shape=jax.ShapeDtypeStruct(pair.shape, BF16),
            in_specs=[pl.BlockSpec(memory_space=pltpu.VMEM)] * 9,
            out_specs=pl.BlockSpec(memory_space=pltpu.VMEM),
            scratch_shapes=[
                pltpu.VMEM((flat, width), F32),
                pltpu.VMEM((flat, width), BF16),
                pltpu.VMEM((flat, width), F32),
                pltpu.VMEM((nc, flat, width), BF16),
                pltpu.VMEM((nr, ratio, cols, cols, width), BF16),
                pltpu.VMEM((nc, cols, cols, width), BF16),
                pltpu.VMEM((nc, rows, cols, width), F32),
                pltpu.VMEM((rows, cols, width), F32),
                dma((nc // 2,)),
                dma((nc // 2,)),
                dma((nc,)),
                dma((nr, ratio, PIECES)),
                dma((nc, PIECES)),
                dma((nr, ratio, PIECES)),
                dma((nr, ratio, PIECES)),
                dma((nr, ratio, PIECES)),
            ],
            compiler_params=pltpu.CompilerParams(collective_id=0, has_side_effects=True),
        )(
            pair, gain_in.reshape(1, -1), w_left_gate, w_left, w_right_gate, w_right,
            gain_out.reshape(1, -1), w_out_gate, w_out,
        )

    return jax.shard_map(
        per_device,
        mesh=mesh,
        in_specs=(P("row", "col", None), P(), P(), P(), P(), P(), P(), P(), P()),
        out_specs=P("row", "col", None),
        check_vma=False,
    )
```

```python
import functools

import jax
import jax.numpy as jnp
from jax import lax
from jax.experimental import pallas as pl
from jax.experimental.pallas import tpu as pltpu
from jax.sharding import PartitionSpec as P

MESH = pl.DeviceIdType.MESH
F32 = jnp.float32
BF16 = jnp.bfloat16
GROUP = 16
PIECES = 1


def layer_norm(values, gain):
    mean = jnp.mean(values, axis=-1, keepdims=True)
    centred = values - mean
    variance = jnp.mean(centred * centred, axis=-1, keepdims=True)
    return centred * lax.rsqrt(variance + 1e-05) * gain


def gated(normed, w_gate, w):
    gate = jnp.dot(normed, w_gate, preferred_element_type=F32)
    value = jnp.dot(normed, w, preferred_element_type=F32)
    return (jax.nn.sigmoid(gate) * value).astype(BF16)


def kernel(
    nr, nc,
    pair, gain_in, w_left_gate, w_left, w_right_gate, w_right, gain_out, w_out_gate, w_out,
    out,
    normed_f, normed_t, gate, left_buf, chain, right_buf, left_f, acc,
    left_send, left_fwd, left_recv, right_send, right_recv, up_send, down_send, chain_recv,
):
    rows, cols, width = pair.shape
    ratio = nc // nr
    chips = nc // 2
    r = lax.axis_index("row")
    c = lax.axis_index("col")
    chip, core = c // 2, c % 2
    depth = cols // PIECES
    parts = [(t, u) for u in range(PIECES) for t in range(ratio)]
    sibling = chip * 2 + 1 - core

    def same_core(a):
        return (chip + a) % chips * 2 + core

    def other_core(a):
        return (chip + a) % chips * 2 + 1 - core

    barrier = pltpu.get_barrier_semaphore()

    def greet(row, col):
        pl.semaphore_signal(barrier, inc=1, device_id={"row": row, "col": col}, device_id_type=MESH)

    for s in range(1, nc):
        greet(r, (c + s) % nc)

    @pl.when(r > 0)
    def _():
        greet(r - 1, c)

    @pl.when(r < nr - 1)
    def _():
        greet(r + 1, c)

    def chain_copy(block, t, u, row, sem):
        piece = chain.at[block, t, pl.ds(u * depth, depth)]
        return pltpu.make_async_remote_copy(
            src_ref=piece, dst_ref=piece, send_sem=sem.at[block, t, u],
            recv_sem=chain_recv.at[block, t, u],
            device_id={"row": row, "col": c}, device_id_type=MESH,
        )

    def right_copy(block, t, u):
        return pltpu.make_async_remote_copy(
            src_ref=chain.at[block, t, pl.ds(u * depth, depth)],
            dst_ref=right_buf.at[c, pl.ds(u * depth, depth)],
            send_sem=right_send.at[block, t, u], recv_sem=right_recv.at[c, u],
            device_id={"row": r, "col": block * ratio + t}, device_id_type=MESH,
        )

    def left_copy(block, col, sem):
        return pltpu.make_async_remote_copy(
            src_ref=left_buf.at[block], dst_ref=left_buf.at[block],
            send_sem=sem, recv_sem=left_recv.at[block],
            device_id={"row": r, "col": col}, device_id_type=MESH,
        )

    def deliver(block, t, u):
        here = block * ratio + t == c

        @pl.when(here)
        def _():
            pltpu.make_async_copy(
                chain.at[block, t, pl.ds(u * depth, depth)],
                right_buf.at[c, pl.ds(u * depth, depth)],
                right_recv.at[c, u],
            ).start()

        @pl.when(jnp.logical_not(here))
        def _():
            right_copy(block, t, u).start()

    normed = layer_norm(pair[...].reshape(rows * cols, width).astype(F32), gain_in[...])
    normed_f[...] = normed
    for t, u in parts:
        for k in range(cols):
            normed_t[pl.ds((t * cols + k) * cols, cols), :] = normed_f[
                pl.ds(t * cols * cols + k, cols, stride=cols), :
            ].astype(BF16)
        block = normed_t[pl.ds(t * cols * cols, cols * cols), :]
        right = gated(block, w_right_gate[...], w_right[...])
        chain[r, t] = right.reshape(cols, cols, width)
        if t == 0:
            pl.semaphore_wait(
                barrier, nc - 1 + (r > 0).astype(jnp.int32) + (r < nr - 1).astype(jnp.int32)
            )

        @pl.when(r < nr - 1)
        def _(t=t, u=u):
            chain_copy(r, t, u, r + 1, up_send).start()

        @pl.when(r > 0)
        def _(t=t, u=u):
            chain_copy(r, t, u, r - 1, down_send).start()

    normed = normed.astype(BF16)
    left_buf[c] = gated(normed, w_left_gate[...], w_left[...])
    for a in range(1, chips):
        left_copy(c, same_core(a), left_send.at[a]).start()
    left_copy(c, sibling, left_send.at[0]).start()

    for t, u in parts:
        deliver(r, t, u)
    gate[...] = jax.nn.sigmoid(jnp.dot(normed, w_out_gate[...], preferred_element_type=F32))
    acc[...] = jnp.zeros_like(acc)

    def widen(block):
        left_f[block] = left_buf[block].astype(F32).reshape(rows, cols, width)

    widen(c)

    def relay(d):
        for t, u in parts:
            @pl.when(r - d >= 0)
            def _(t=t, u=u):
                block = r - d
                chain_copy(block, t, u, r, up_send).wait_recv()

                @pl.when(r < nr - 1)
                def _():
                    chain_copy(block, t, u, r + 1, up_send).start()

                deliver(block, t, u)

            @pl.when(r + d < nr)
            def _(t=t, u=u):
                block = r + d
                chain_copy(block, t, u, r, down_send).wait_recv()

                @pl.when(r > 0)
                def _():
                    chain_copy(block, t, u, r - 1, down_send).start()

                deliver(block, t, u)

    for d in range(1, nr - 1):
        relay(d)
    for a in range(1, chips):
        block = same_core(a)
        left_copy(block, sibling, left_fwd.at[a]).wait_recv()
        left_copy(block, sibling, left_fwd.at[a]).start()
        widen(block)
    relay(nr - 1)
    for a in range(chips):
        block = other_core(a)
        left_copy(block, sibling, left_send.at[0]).wait_recv()
        widen(block)

    def mix(block, u):
        pltpu.make_async_remote_copy(
            src_ref=chain.at[0, 0, pl.ds(0, depth)],
            dst_ref=right_buf.at[block, pl.ds(u * depth, depth)],
            send_sem=right_send.at[0, 0, 0], recv_sem=right_recv.at[block, u],
            device_id={"row": r, "col": sibling}, device_id_type=MESH,
        ).wait_recv()

        def group(g, carry):
            sums = [acc[g * GROUP + n] for n in range(GROUP)]
            for k in range(u * depth, (u + 1) * depth):
                other = right_buf[block, k].astype(F32)
                for n in range(GROUP):
                    sums[n] = sums[n] + left_f[block, g * GROUP + n, pl.ds(k, 1), :] * other
            for n in range(GROUP):
                acc[g * GROUP + n] = sums[n]
            return carry

        lax.fori_loop(0, rows // GROUP, group, 0)

    for u in range(PIECES):
        def step(s, carry, u=u):
            mix((chip + s // 2) % chips * 2 + (core + s) % 2, u)
            return carry

        lax.fori_loop(0, nc, step, 0)

    mixed = acc[...].reshape(rows * cols, width)
    out_normed = layer_norm(mixed, gain_out[...]).astype(BF16)
    update = gate[...] * jnp.dot(out_normed, w_out[...], preferred_element_type=F32)
    out[...] = update.astype(BF16).reshape(rows, cols, width)

    left_copy(c, sibling, left_send.at[0]).wait_send()
    for a in range(1, chips):
        left_copy(c, same_core(a), left_send.at[a]).wait_send()
        left_copy(same_core(a), sibling, left_fwd.at[a]).wait_send()
    for block in range(nr):
        for t, u in parts:
            @pl.when(block * ratio + t != c)
            def _(block=block, t=t, u=u):
                right_copy(block, t, u).wait_send()

            @pl.when(jnp.logical_and(r >= block, r < nr - 1))
            def _(block=block, t=t, u=u):
                chain_copy(block, t, u, r + 1, up_send).wait_send()

            @pl.when(jnp.logical_and(r <= block, r > 0))
            def _(block=block, t=t, u=u):
                chain_copy(block, t, u, r - 1, down_send).wait_send()


def solution(mesh):
    nr, nc = mesh.shape["row"], mesh.shape["col"]

    def per_device(
        pair, gain_in, w_left_gate, w_left, w_right_gate, w_right, gain_out, w_out_gate, w_out
    ):
        rows, cols, width = pair.shape
        flat = rows * cols
        ratio = nc // nr
        dma = pltpu.SemaphoreType.DMA
        return pl.pallas_call(
            functools.partial(kernel, nr, nc),
            out_shape=jax.ShapeDtypeStruct(pair.shape, BF16),
            in_specs=[pl.BlockSpec(memory_space=pltpu.VMEM)] * 9,
            out_specs=pl.BlockSpec(memory_space=pltpu.VMEM),
            scratch_shapes=[
                pltpu.VMEM((flat, width), F32),
                pltpu.VMEM((flat, width), BF16),
                pltpu.VMEM((flat, width), F32),
                pltpu.VMEM((nc, flat, width), BF16),
                pltpu.VMEM((nr, ratio, cols, cols, width), BF16),
                pltpu.VMEM((nc, cols, cols, width), BF16),
                pltpu.VMEM((nc, rows, cols, width), F32),
                pltpu.VMEM((rows, cols, width), F32),
                dma((nc // 2,)),
                dma((nc // 2,)),
                dma((nc,)),
                dma((nr, ratio, PIECES)),
                dma((nc, PIECES)),
                dma((nr, ratio, PIECES)),
                dma((nr, ratio, PIECES)),
                dma((nr, ratio, PIECES)),
            ],
            compiler_params=pltpu.CompilerParams(collective_id=0, has_side_effects=True),
        )(
            pair, gain_in.reshape(1, -1), w_left_gate, w_left, w_right_gate, w_right,
            gain_out.reshape(1, -1), w_out_gate, w_out,
        )

    return jax.shard_map(
        per_device,
        mesh=mesh,
        in_specs=(P("row", "col", None), P(), P(), P(), P(), P(), P(), P(), P()),
        out_specs=P("row", "col", None),
        check_vma=False,
    )
```
